32 devices in a mesh: gx: 4 (over y, x), gy: 4 (over z), side: 2 (over core).
Axes of the slice: x: 2, y: 2, z: 4, core: 2. Of those that a mesh axis runs over, the one named last changes fastest.
Arguments:
- source: float32 [2, 4, 256, 512], P('side', None, 'gx', 'gy'), may hold values from -20 to 20
- classes: int32 [2, 4, 256, 512], P('side', None, 'gx', 'gy'), may hold values from 0 to 7
- table: float32 [2, 8, 3], replicated, may hold values from 0.1 to 10
Outputs:
- solution: float32 [2, 4, 256, 512], P('side', None, 'gx', 'gy')
- trace_change: float32 [2], replicated
The draws below stay inside these ranges and needn't reach their ends.
All inputs are finite; a program needn't handle non-finite values.
Results may differ from the reference program's by a relative error of at most 0.0001.
Values sent between devices are 32-bit elements; how exact they have to be, the bound alone decides.
A program may use at most 64 MiB of HBM per device.

```python
import math
import jax
import jax.numpy as jnp

LAYERS = 4
SWEEPS = 8
ITERS = 2
NCLASS = 8
NX = 256
NY = 512


def draw_source(key, part):
    shape = (2, LAYERS, NX, NY)
    position = jnp.arange(NX, dtype=jnp.float32) / max(NX - 1, 1)
    ramp = jnp.exp(jnp.log(3.0) * position)[None, None, :, None]
    return jnp.clip(jax.random.normal(key, shape, jnp.float32), -6.0, 6.0) * ramp


def with_ends(values, stream_key, least, high):
    longest = values.shape.index(max(values.shape))
    spots = []
    for shift in (0, 1):
        where = [jax.random.randint(jax.random.fold_in(stream_key, axis), (), 0, length) for axis, length in enumerate(values.shape)]
        where[longest] = (where[longest] + shift) % values.shape[longest]
        spots.append(tuple(where))
    return values.at[spots[0]].set(least).at[spots[1]].set(high)


def setup_inputs(seed: int = 0) -> dict:
    key_list = jax.random.split(jax.random.key(seed), 4)
    source = draw_source(jax.random.fold_in(key_list[3], 71), 0)
    classes = with_ends(jax.random.randint(key_list[1], (2, LAYERS, NX, NY), 0, NCLASS), jax.random.fold_in(key_list[1], 1), 0, NCLASS - 1).astype(jnp.int32)
    table = jnp.clip(jnp.exp(jax.random.uniform(key_list[2], (2, NCLASS, 3), jnp.float32, math.log(0.1), math.log(10.0))), 0.1, 10.0)
    return {"source": source, "classes": classes, "table": table}


relax_weight = 0.8
robin_weight = 2.0

def lookup(classes, table, column):
    result = jnp.zeros(classes.shape, jnp.float32)
    for level in range(NCLASS):
        values = table[:, level, column][:, None, None, None]
        result = jnp.where(classes == level, values, result)
    return result

def relax(field, robin_data, source, cond_x, cond_y, cond_z, diagonal):
    padded = jnp.pad(field, ((0, 0), (1, 1), (1, 1), (1, 1)))
    beside = cond_x * (padded[:, 1:-1, 2:, 1:-1] + padded[:, 1:-1, :-2, 1:-1])
    beside = beside + cond_y * (padded[:, 1:-1, 1:-1, 2:] + padded[:, 1:-1, 1:-1, :-2])
    beside = beside + cond_z * (padded[:, 2:, 1:-1, 1:-1] + padded[:, :-2, 1:-1, 1:-1])
    total = source + beside
    total = total.at[:, 0].add(robin_data)
    return (1.0 - relax_weight) * field + relax_weight * total / diagonal

def reference(source, classes, table):
    cond_x = lookup(classes, table, 0)
    cond_y = lookup(classes, table, 1)
    cond_z = lookup(classes, table, 2)
    diagonal = 2.0 * (cond_x + cond_y + cond_z)
    diagonal = diagonal.at[:, 0].add(robin_weight)
    field = jnp.zeros(source.shape, jnp.float32)
    robin_data = jnp.zeros((2, source.shape[2], source.shape[3]), jnp.float32)
    changes = []
    for outer in range(ITERS):
        for inner in range(SWEEPS):
            field = relax(field, robin_data, source, cond_x, cond_y, cond_z, diagonal)
        outgoing = robin_weight * field[:, 0] - robin_data
        new_data = outgoing[::-1]
        changes.append(jnp.sqrt(jnp.sum((new_data - robin_data) ** 2)))
        robin_data = new_data
    return (field, jnp.stack(changes))
```

```python
import functools

import jax
import jax.numpy as jnp
from jax import lax
from jax.experimental import pallas as pl
from jax.experimental.pallas import tpu as pltpu
from jax.sharding import PartitionSpec as P

SWEEPS = 8
ITERS = 2
NCLASS = 8
REACH = SWEEPS * ITERS

relax_weight = 0.8
robin_weight = 2.0

MESH = pl.DeviceIdType.MESH
AXES = ("gx", "gy", "side")
AROUND = [(dx, dy) for dx in (-1, 0, 1) for dy in (-1, 0, 1) if (dx, dy) != (0, 0)]


def reduce_groups(sizes):
    return [("gx", "side"), ("gy",)]


def kernel(
    sizes,
    source_hbm,
    classes_hbm,
    table,
    out_hbm,
    trace,
    src,
    cls,
    pack,
    halo,
    cond,
    field,
    weight,
    mine,
    theirs,
    *rest,
):
    groups = reduce_groups(sizes)
    sums = rest[: len(groups)]
    partial, local_sem, send_sem, recv_sem, side_sem, sum_send, sum_recv, out_sem = rest[len(groups) :]
    layers, rows, lanes = source_hbm.shape[1:]
    wide = rows + 2 * REACH
    gx, gy, side = (lax.axis_index(axis) for axis in AXES)
    at = {"gx": gx, "gy": gy, "side": side}

    def exists(dx, dy):
        ok = None
        for d, axis in ((dx, "gx"), (dy, "gy")):
            if d:
                here = at[axis] > 0 if d < 0 else at[axis] < sizes[axis] - 1
                ok = here if ok is None else ok & here
        return ok

    def members(group):
        count = 1
        for axis in group:
            count *= sizes[axis]
        index = 0
        for axis in group:
            index = index * sizes[axis] + at[axis]
        for step in range(1, count):
            other = lax.rem(index + step, count)
            place = dict(at)
            left = other
            for axis in reversed(group):
                place[axis] = lax.rem(left, sizes[axis])
                left = left // sizes[axis]
            yield tuple(place[axis] for axis in AXES)

    middle = pl.ds(REACH, rows)
    load_src = pltpu.make_async_copy(source_hbm.at[0], src.at[:, middle], local_sem.at[0])
    load_cls = pltpu.make_async_copy(classes_hbm.at[0], cls.at[:, middle], local_sem.at[1])
    load_src.start()
    load_cls.start()

    barrier = pltpu.get_barrier_semaphore()
    expected = 1
    pl.semaphore_signal(barrier, inc=1, device_id=(gx, gy, 1 - side), device_id_type=MESH)
    for dx, dy in AROUND:
        ok = exists(dx, dy)
        expected = expected + ok.astype(jnp.int32)

        @pl.when(ok)
        def _():
            pl.semaphore_signal(barrier, inc=1, device_id=(gx + dx, gy + dy, side), device_id_type=MESH)

    for group in groups:
        for peer in members(group):
            pl.semaphore_signal(barrier, inc=1, device_id=peer, device_id_type=MESH)
            expected = expected + 1

    lane = lax.broadcasted_iota(jnp.int32, (8, lanes), 1)
    low = lax.broadcasted_iota(jnp.int32, (8, lanes), 0)
    scalars = [[table[side, level, column] for column in range(3)] for level in range(NCLASS)]
    columns = []
    for column in range(3):
        value = jnp.zeros((8, lanes), jnp.float32)
        for level in range(NCLASS):
            value = jnp.where(lane == level, scalars[level][column], value)
        columns.append(value)
    doubled = 2.0 * (columns[0] + columns[1] + columns[2])
    doubled = jnp.where(lane < NCLASS, doubled, 1.0)
    tables = []
    for extra in (robin_weight, 0.0):
        share = relax_weight / (doubled + extra)
        tables.append([share * column for column in columns] + [share])

    load_src.wait()
    load_cls.wait()

    lane_wide = lax.broadcasted_iota(jnp.int32, (rows, lanes), 1)
    for way, first in ((0, 0), (1, lanes - REACH)):
        packed = jnp.zeros((rows, lanes), jnp.float32)
        for strip in range(2 * layers):
            ref = src if strip < layers else cls
            value = ref[strip % layers, middle, :].astype(jnp.float32)
            shift = (strip * REACH - first) % lanes
            if shift:
                value = pltpu.roll(value, shift, 1)
            packed = jnp.where(lane_wide // REACH == strip, value, packed)
        pack[way] = packed

    pl.semaphore_wait(barrier, expected)

    copies = []

    def send(condition, source_ref, target_ref, peer):
        number = len(copies)
        copy = pltpu.make_async_remote_copy(
            src_ref=source_ref,
            dst_ref=target_ref,
            send_sem=send_sem.at[number],
            recv_sem=recv_sem.at[number],
            device_id=peer,
            device_id_type=MESH,
        )
        copies.append((condition, copy))

        @pl.when(condition)
        def _():
            copy.start()

    def strip_of(dx):
        if dx == 0:
            return middle, pl.ds(0, rows), middle
        if dx > 0:
            return pl.ds(rows, REACH), pl.ds(rows - REACH, REACH), pl.ds(0, REACH)
        return pl.ds(REACH, REACH), pl.ds(0, REACH), pl.ds(REACH + rows, REACH)

    arrive = []
    for dx, dy in sorted(AROUND, key=lambda d: -abs(d[0]) - abs(d[1])):
        held, inner, landing = strip_of(dx)
        peer = (gx + dx, gy + dy, side)
        arrive.append(exists(-dx, -dy))
        if dy == 0:
            send(exists(dx, dy), src.at[:, held], src.at[:, landing], peer)
            arrive.append(exists(-dx, -dy))
            send(exists(dx, dy), cls.at[:, held], cls.at[:, landing], peer)
        elif dy > 0:
            send(exists(dx, dy), pack.at[1, inner], halo.at[0, landing], peer)
        else:
            send(exists(dx, dy), pack.at[0, inner], halo.at[1, landing], peer)

    def lookup(kinds, wanted):
        chosen = []
        for row in wanted:
            chosen.append(jnp.take_along_axis(jnp.broadcast_to(row[:1], kinds.shape), kinds, axis=1))
        return chosen

    def settle(part, layer, span, kinds, values, ok):
        count = span.size
        wanted = lookup(kinds, tables[0 if layer == 0 else 1])
        wanted[3], values = wanted[3], wanted[3] * values
        if ok is not None:
            wanted = [jnp.where(ok, value, 0.0) for value in wanted]
            values = jnp.where(ok, values, 0.0)
        for number in range(3):
            cond[number, part, layer, span] = wanted[number]
        cond[3, part, layer, span] = values
        field[1, part, layer + 1, span] = values
        if layer == 0:
            weight[part, span] = wanted[3]

    zero = jnp.zeros((wide, lanes), jnp.float32)
    for slot in range(2):
        for part in range(2):
            field[slot, part, 0] = zero
            field[slot, part, layers + 1] = zero

    for layer in range(layers):
        settle(0, layer, middle, cls[layer, middle, :], src[layer, middle, :], None)

    for (condition, copy), here in zip(copies, arrive):

        @pl.when(here)
        def _():
            copy.wait_recv()

    for dx in (-1, 1):
        span = pl.ds(0, REACH) if dx < 0 else pl.ds(REACH + rows, REACH)
        there = exists(dx, 0)
        ok = jnp.broadcast_to(there, (REACH, lanes))
        for layer in range(layers):
            settle(0, layer, span, jnp.where(ok, cls[layer, span, :], 0), src[layer, span, :], ok)

    row = lax.broadcasted_iota(jnp.int32, (wide, lanes), 0)
    wide_lane = lax.broadcasted_iota(jnp.int32, (wide, lanes), 1)
    ok_rows = ((row >= REACH) | (gx > 0)) & ((row < REACH + rows) | (gx < sizes["gx"] - 1))
    ok_left = ok_rows & (wide_lane >= lanes - REACH) & (gy > 0)
    ok_right = ok_rows & (wide_lane < REACH) & (gy < sizes["gy"] - 1)
    ok_wide = ok_left | ok_right
    halo_left = halo[0]
    halo_right = halo[1]
    everything = pl.ds(0, wide)
    for layer in range(layers):
        found = []
        for strip in (layer, layers + layer):
            left = pltpu.roll(halo_left, (lanes - REACH - strip * REACH) % lanes, 1)
            right = pltpu.roll(halo_right, (-strip * REACH) % lanes, 1) if strip else halo_right
            found.append(jnp.where(ok_left, left, jnp.where(ok_right, right, 0.0)))
        settle(1, layer, everything, found[1].astype(jnp.int32), found[0], ok_wide)

    def relax(time, layer, first, count, parts=2):
        old, new = (time - 1) % 2, time % 2
        span = pl.ds(first, count)
        edge = lax.broadcasted_iota(jnp.int32, (count, lanes), 1)
        grow = REACH if parts == 1 else 0
        before = [field[old, part, layer + 1, span] for part in range(2)]
        from_left = [pltpu.roll(value, 1, 1) for value in before]
        from_right = [pltpu.roll(value, lanes - 1, 1) for value in before]
        for part in range(parts):
            here = before[part]
            if parts == 1:
                outer = field[old, part, layer + 1, pl.ds(first - 8, count + 16)]
                above = pltpu.roll(outer, 1, 0)[8 : 8 + count]
                below = pltpu.roll(outer, count + 15, 0)[8 : 8 + count]
            else:
                above = pltpu.roll(here, 1, 0)
                below = pltpu.roll(here, count - 1, 0)
            left = jnp.where(edge == 0, from_left[1 - part], from_left[part])
            right = jnp.where(edge == lanes - 1, from_right[1 - part], from_right[part])
            deep = field[old, part, layer, span] + field[old, part, layer + 2, span]
            value = (1.0 - relax_weight) * here + cond[3, part, layer, span]
            value = value + cond[0, part, layer, span] * (above + below)
            value = value + cond[1, part, layer, span] * (left + right)
            value = value + cond[2, part, layer, span] * deep
            field[new, part, layer + 1, span] = value

    def sweep(time, layer):
        if time <= SWEEPS:
            relax(time, layer, 0, wide)
        elif time < REACH:
            relax(time, layer, SWEEPS, wide - 2 * SWEEPS)
        else:
            relax(time, layer, REACH, rows, parts=1)

    def full(start, pairs):
        @pl.loop(0, pairs)
        def _(_):
            for time in (start, start + 1):
                for layer in range(layers):
                    sweep(time, layer)

    def head(last):
        for depth in range(layers - 1):
            time = last - (layers - 2) + depth
            for layer in range(layers - 1 - depth):
                sweep(time, layer)

    def tail(last):
        for step in range(layers - 1):
            for layer in range(layers - 1, step, -1):
                sweep(last - layer + 1 + step, layer)

    full(2, 2)
    head(SWEEPS)
    near = pl.ds(SWEEPS, wide - 2 * SWEEPS)
    for part in range(2):
        mine[part] = robin_weight * field[0, part, 1, near]
    across = pltpu.make_async_remote_copy(
        src_ref=mine,
        dst_ref=theirs,
        send_sem=side_sem.at[0],
        recv_sem=side_sem.at[1],
        device_id=(gx, gy, 1 - side),
        device_id_type=MESH,
    )
    across.start()
    tail(SWEEPS)

    for depth in range(layers - 1):
        for layer in range(1 + depth, layers):
            sweep(SWEEPS + 1 + depth, layer)
    across.wait_recv()
    for part in range(2):
        cond[3, part, 0, near] = cond[3, part, 0, near] + weight[part, near] * theirs[part]
    for depth in range(layers - 1):
        for layer in range(layers - 1 - depth):
            sweep(SWEEPS + 1 + depth + layer, layer)
    full(SWEEPS + layers, 1)
    head(REACH)

    inner = pl.ds(SWEEPS, rows)
    first_change = mine[0, inner]
    own = robin_weight * field[0, 0, 1, middle]
    second_change = own - theirs[0, inner] - first_change
    folded = []
    for change in (first_change, second_change):
        square = jnp.sum((change * change).reshape(rows // 8, 8, lanes), axis=0)
        folded.append(square + pltpu.roll(square, 4, 0))
    total = jnp.where(low < 4, folded[0], folded[1])

    def exchange(number):
        group = groups[number]
        slots = sums[number]
        peers = list(members(group))
        started = []
        for k, peer in enumerate(peers):
            copy = pltpu.make_async_remote_copy(
                src_ref=partial.at[number],
                dst_ref=slots.at[k],
                send_sem=sum_send.at[number, k],
                recv_sem=sum_recv.at[number, k],
                device_id=peer,
                device_id_type=MESH,
            )
            copy.start()
            started.append(copy)
        return started

    partial[0] = total
    started = exchange(0)
    tail(REACH)
    written = pltpu.make_async_copy(field.at[0, 0, pl.ds(1, layers), middle], out_hbm.at[0], out_sem)
    written.start()
    for number in range(len(groups)):
        for k, copy in enumerate(started):
            copy.wait_recv()
            total = total + sums[number][k]
        for copy in started:
            copy.wait_send()
        if number + 1 < len(groups):
            partial[number + 1] = total
            started = exchange(number + 1)
    for number in range(ITERS):
        part = jnp.sum(jnp.where(low // 4 == number, total, 0.0))
        root = jnp.sqrt(jnp.broadcast_to(part, (8, lanes)))
        trace[number] = root[0, 0]

    for condition, copy in copies:

        @pl.when(condition)
        def _():
            copy.wait_send()

    across.wait_send()
    written.wait()


def on_device(sizes, source, classes, table):
    layers, rows, lanes = source.shape[1:]
    wide = rows + 2 * REACH
    groups = reduce_groups(sizes)
    counts = []
    for group in groups:
        count = 1
        for axis in group:
            count *= sizes[axis]
        counts.append(count)
    near = wide - 2 * SWEEPS
    return pl.pallas_call(
        functools.partial(kernel, sizes),
        out_shape=(
            jax.ShapeDtypeStruct(source.shape, jnp.float32),
            jax.ShapeDtypeStruct((ITERS,), jnp.float32),
        ),
        in_specs=[
            pl.BlockSpec(memory_space=pl.ANY),
            pl.BlockSpec(memory_space=pl.ANY),
            pl.BlockSpec(memory_space=pltpu.SMEM),
        ],
        out_specs=(
            pl.BlockSpec(memory_space=pl.ANY),
            pl.BlockSpec(memory_space=pltpu.SMEM),
        ),
        scratch_shapes=[
            pltpu.VMEM((layers, wide, lanes), jnp.float32),
            pltpu.VMEM((layers, wide, lanes), jnp.int32),
            pltpu.VMEM((2, rows, lanes), jnp.float32),
            pltpu.VMEM((2, wide, lanes), jnp.float32),
            pltpu.VMEM((4, 2, layers, wide, lanes), jnp.float32),
            pltpu.VMEM((2, 2, layers + 2, wide, lanes), jnp.float32),
            pltpu.VMEM((2, wide, lanes), jnp.float32),
            pltpu.VMEM((2, near, lanes), jnp.float32),
            pltpu.VMEM((2, near, lanes), jnp.float32),
            *[pltpu.VMEM((count - 1, 8, lanes), jnp.float32) for count in counts],
            pltpu.VMEM((len(groups), 8, lanes), jnp.float32),
            pltpu.SemaphoreType.DMA((2,)),
            pltpu.SemaphoreType.DMA((10,)),
            pltpu.SemaphoreType.DMA((10,)),
            pltpu.SemaphoreType.DMA((2,)),
            pltpu.SemaphoreType.DMA((len(groups), max(counts))),
            pltpu.SemaphoreType.DMA((len(groups), max(counts))),
            pltpu.SemaphoreType.DMA,
        ],
        compiler_params=pltpu.CompilerParams(
            collective_id=0, has_side_effects=True, vmem_limit_bytes=48 * 2**20
        ),
    )(source, classes, table)


def solution(mesh):
    sizes = {axis: mesh.shape[axis] for axis in AXES}
    in_specs = (P("side", None, "gx", "gy"), P("side", None, "gx", "gy"), P())
    out_specs = (P("side", None, "gx", "gy"), P())
    return jax.shard_map(
        functools.partial(on_device, sizes),
        mesh=mesh,
        in_specs=in_specs,
        out_specs=out_specs,
        check_vma=False,
    )
```

```python
import functools

import jax
import jax.numpy as jnp
from jax import lax
from jax.experimental import pallas as pl
from jax.experimental.pallas import tpu as pltpu
from jax.sharding import PartitionSpec as P

SWEEPS = 8
ITERS = 2
NCLASS = 8
REACH = SWEEPS * ITERS

relax_weight = 0.8
robin_weight = 2.0

MESH = pl.DeviceIdType.MESH
AXES = ("gx", "gy", "side")
AROUND = [(dx, dy) for dx in (-1, 0, 1) for dy in (-1, 0, 1) if (dx, dy) != (0, 0)]


def reduce_groups(sizes):
    return [("gy", "side"), ("gx",)]


def kernel(
    sizes,
    source_hbm,
    classes_hbm,
    table_hbm,
    out_hbm,
    trace,
    src,
    cls,
    pack,
    halo,
    cond,
    field,
    weight,
    mine,
    theirs,
    *rest,
):
    groups = reduce_groups(sizes)
    sums = rest[: len(groups)]
    partial, table, local_sem, send_sem, recv_sem, side_sem, sum_send, sum_recv, out_sem = rest[len(groups) :]
    layers, rows, lanes = source_hbm.shape[1:]
    wide = rows + 2 * REACH
    gx, gy, side = (lax.axis_index(axis) for axis in AXES)
    at = {"gx": gx, "gy": gy, "side": side}

    def exists(dx, dy):
        ok = None
        for d, axis in ((dx, "gx"), (dy, "gy")):
            if d:
                here = at[axis] > 0 if d < 0 else at[axis] < sizes[axis] - 1
                ok = here if ok is None else ok & here
        return ok

    def members(group):
        count = 1
        for axis in group:
            count *= sizes[axis]
        index = 0
        for axis in group:
            index = index * sizes[axis] + at[axis]
        for step in range(1, count):
            other = lax.rem(index + step, count)
            place = dict(at)
            left = other
            for axis in reversed(group):
                place[axis] = lax.rem(left, sizes[axis])
                left = left // sizes[axis]
            yield tuple(place[axis] for axis in AXES)

    load_table = pltpu.make_async_copy(table_hbm, table, local_sem.at[2])
    load_table.start()
    middle = pl.ds(REACH, rows)
    load_src = pltpu.make_async_copy(source_hbm.at[0], src.at[:, middle], local_sem.at[0])
    load_cls = pltpu.make_async_copy(classes_hbm.at[0], cls.at[:, middle], local_sem.at[1])
    load_src.start()
    load_cls.start()

    barrier = pltpu.get_barrier_semaphore()
    expected = 1
    pl.semaphore_signal(barrier, inc=1, device_id=(gx, gy, 1 - side), device_id_type=MESH)
    for dx, dy in AROUND:
        ok = exists(dx, dy)
        expected = expected + ok.astype(jnp.int32)

        @pl.when(ok)
        def _():
            pl.semaphore_signal(barrier, inc=1, device_id=(gx + dx, gy + dy, side), device_id_type=MESH)

    for group in groups:
        for peer in members(group):
            pl.semaphore_signal(barrier, inc=1, device_id=peer, device_id_type=MESH)
            expected = expected + 1

    lane = lax.broadcasted_iota(jnp.int32, (8, lanes), 1)
    low = lax.broadcasted_iota(jnp.int32, (8, lanes), 0)
    load_table.wait()
    scalars = [[table[column, side, level] for column in range(3)] for level in range(NCLASS)]
    columns = []
    for column in range(3):
        value = jnp.zeros((8, lanes), jnp.float32)
        for level in range(NCLASS):
            value = jnp.where(lane == level, scalars[level][column], value)
        columns.append(value)
    doubled = 2.0 * (columns[0] + columns[1] + columns[2])
    doubled = jnp.where(lane < NCLASS, doubled, 1.0)
    tables = []
    for extra in (robin_weight, 0.0):
        share = relax_weight / (doubled + extra)
        tables.append([share * column for column in columns] + [share])

    load_src.wait()
    load_cls.wait()

    lane_wide = lax.broadcasted_iota(jnp.int32, (rows, lanes), 1)
    for way, first in ((0, 0), (1, lanes - REACH)):
        packed = jnp.zeros((rows, lanes), jnp.float32)
        for strip in range(2 * layers):
            ref = src if strip < layers else cls
            value = ref[strip % layers, middle, :].astype(jnp.float32)
            shift = (strip * REACH - first) % lanes
            if shift:
                value = pltpu.roll(value, shift, 1)
            packed = jnp.where(lane_wide // REACH == strip, value, packed)
        pack[way] = packed

    pl.semaphore_wait(barrier, expected)

    copies = []

    def send(condition, source_ref, target_ref, peer):
        number = len(copies)
        copy = pltpu.make_async_remote_copy(
            src_ref=source_ref,
            dst_ref=target_ref,
            send_sem=send_sem.at[number],
            recv_sem=recv_sem.at[number],
            device_id=peer,
            device_id_type=MESH,
        )
        copies.append((condition, copy))

        @pl.when(condition)
        def _():
            copy.start()

    def strip_of(dx):
        if dx == 0:
            return middle, pl.ds(0, rows), middle
        if dx > 0:
            return pl.ds(rows, REACH), pl.ds(rows - REACH, REACH), pl.ds(0, REACH)
        return pl.ds(REACH, REACH), pl.ds(0, REACH), pl.ds(REACH + rows, REACH)

    arrive = []
    for dx, dy in sorted(AROUND, key=lambda d: -abs(d[0]) - abs(d[1])):
        held, inner, landing = strip_of(dx)
        peer = (gx + dx, gy + dy, side)
        arrive.append(exists(-dx, -dy))
        if dy == 0:
            send(exists(dx, dy), src.at[:, held], src.at[:, landing], peer)
            arrive.append(exists(-dx, -dy))
            send(exists(dx, dy), cls.at[:, held], cls.at[:, landing], peer)
        elif dy > 0:
            send(exists(dx, dy), pack.at[1, inner], halo.at[0, landing], peer)
        else:
            send(exists(dx, dy), pack.at[0, inner], halo.at[1, landing], peer)

    def lookup(kinds, wanted):
        chosen = []
        for row in wanted:
            chosen.append(jnp.take_along_axis(jnp.broadcast_to(row[:1], kinds.shape), kinds, axis=1))
        return chosen

    def settle(part, layer, span, kinds, values, ok):
        count = span.size
        wanted = lookup(kinds, tables[0 if layer == 0 else 1])
        wanted[3], values = wanted[3], wanted[3] * values
        if ok is not None:
            wanted = [jnp.where(ok, value, 0.0) for value in wanted]
            values = jnp.where(ok, values, 0.0)
        for number in range(3):
            cond[number, part, layer, span] = wanted[number]
        cond[3, part, layer, span] = values
        field[1, part, layer + 1, span] = values
        if layer == 0:
            weight[part, span] = wanted[3]

    zero = jnp.zeros((wide, lanes), jnp.float32)
    for slot in range(2):
        for part in range(2):
            field[slot, part, 0] = zero
            field[slot, part, layers + 1] = zero

    for layer in range(layers):
        settle(0, layer, middle, cls[layer, middle, :], src[layer, middle, :], None)

    for (condition, copy), here in zip(copies, arrive):

        @pl.when(here)
        def _():
            copy.wait_recv()

    for dx in (-1, 1):
        span = pl.ds(0, REACH) if dx < 0 else pl.ds(REACH + rows, REACH)
        there = exists(dx, 0)
        ok = jnp.broadcast_to(there, (REACH, lanes))
        for layer in range(layers):
            settle(0, layer, span, jnp.where(ok, cls[layer, span, :], 0), src[layer, span, :], ok)

    row = lax.broadcasted_iota(jnp.int32, (wide, lanes), 0)
    wide_lane = lax.broadcasted_iota(jnp.int32, (wide, lanes), 1)
    ok_rows = ((row >= REACH) | (gx > 0)) & ((row < REACH + rows) | (gx < sizes["gx"] - 1))
    ok_left = ok_rows & (wide_lane >= lanes - REACH) & (gy > 0)
    ok_right = ok_rows & (wide_lane < REACH) & (gy < sizes["gy"] - 1)
    ok_wide = ok_left | ok_right
    halo_left = halo[0]
    halo_right = halo[1]
    everything = pl.ds(0, wide)
    for layer in range(layers):
        found = []
        for strip in (layer, layers + layer):
            left = pltpu.roll(halo_left, (lanes - REACH - strip * REACH) % lanes, 1)
            right = pltpu.roll(halo_right, (-strip * REACH) % lanes, 1) if strip else halo_right
            found.append(jnp.where(ok_left, left, jnp.where(ok_right, right, 0.0)))
        settle(1, layer, everything, found[1].astype(jnp.int32), found[0], ok_wide)

    def relax(time, layer, first, count, parts=2):
        old, new = (time - 1) % 2, time % 2
        span = pl.ds(first, count)
        edge = lax.broadcasted_iota(jnp.int32, (count, lanes), 1)
        grow = REACH if parts == 1 else 0
        before = [field[old, part, layer + 1, span] for part in range(2)]
        from_left = [pltpu.roll(value, 1, 1) for value in before]
        from_right = [pltpu.roll(value, lanes - 1, 1) for value in before]
        for part in range(parts):
            here = before[part]
            if parts == 1:
                outer = field[old, part, layer + 1, pl.ds(first - 8, count + 16)]
                above = pltpu.roll(outer, 1, 0)[8 : 8 + count]
                below = pltpu.roll(outer, count + 15, 0)[8 : 8 + count]
            else:
                above = pltpu.roll(here, 1, 0)
                below = pltpu.roll(here, count - 1, 0)
            left = jnp.where(edge == 0, from_left[1 - part], from_left[part])
            right = jnp.where(edge == lanes - 1, from_right[1 - part], from_right[part])
            deep = field[old, part, layer, span] + field[old, part, layer + 2, span]
            value = (1.0 - relax_weight) * here + cond[3, part, layer, span]
            value = value + cond[0, part, layer, span] * (above + below)
            value = value + cond[1, part, layer, span] * (left + right)
            value = value + cond[2, part, layer, span] * deep
            field[new, part, layer + 1, span] = value

    def sweep(time, layer):
        if time <= SWEEPS:
            relax(time, layer, 0, wide)
        elif time < REACH:
            relax(time, layer, SWEEPS, wide - 2 * SWEEPS)
        else:
            relax(time, layer, REACH, rows, parts=1)

    def full(start, pairs):
        @pl.loop(0, pairs)
        def _(_):
            for time in (start, start + 1):
                for layer in range(layers):
                    sweep(time, layer)

    def head(last):
        for depth in range(layers - 1):
            time = last - (layers - 2) + depth
            for layer in range(layers - 1 - depth):
                sweep(time, layer)

    def tail(last):
        for step in range(layers - 1):
            for layer in range(layers - 1, step, -1):
                sweep(last - layer + 1 + step, layer)

    full(2, 2)
    head(SWEEPS)
    near = pl.ds(SWEEPS, wide - 2 * SWEEPS)
    for part in range(2):
        mine[part] = robin_weight * field[0, part, 1, near]
    across = pltpu.make_async_remote_copy(
        src_ref=mine,
        dst_ref=theirs,
        send_sem=side_sem.at[0],
        recv_sem=side_sem.at[1],
        device_id=(gx, gy, 1 - side),
        device_id_type=MESH,
    )
    across.start()
    tail(SWEEPS)

    for depth in range(layers - 1):
        for layer in range(1 + depth, layers):
            sweep(SWEEPS + 1 + depth, layer)
    across.wait_recv()
    for part in range(2):
        cond[3, part, 0, near] = cond[3, part, 0, near] + weight[part, near] * theirs[part]
    for depth in range(layers - 1):
        for layer in range(layers - 1 - depth):
            sweep(SWEEPS + 1 + depth + layer, layer)
    full(SWEEPS + layers, 1)
    head(REACH)

    inner = pl.ds(SWEEPS, rows)
    first_change = mine[0, inner]
    own = robin_weight * field[0, 0, 1, middle]
    second_change = own - theirs[0, inner] - first_change
    folded = []
    for change in (first_change, second_change):
        square = jnp.sum((change * change).reshape(rows // 8, 8, lanes), axis=0)
        folded.append(square + pltpu.roll(square, 4, 0))
    total = jnp.where(low < 4, folded[0], folded[1])

    def exchange(number):
        group = groups[number]
        slots = sums[number]
        peers = list(members(group))
        started = []
        for k, peer in enumerate(peers):
            copy = pltpu.make_async_remote_copy(
                src_ref=partial.at[number],
                dst_ref=slots.at[k],
                send_sem=sum_send.at[number, k],
                recv_sem=sum_recv.at[number, k],
                device_id=peer,
                device_id_type=MESH,
            )
            copy.start()
            started.append(copy)
        return started

    partial[0] = total
    started = exchange(0)
    tail(REACH)
    written = pltpu.make_async_copy(field.at[0, 0, pl.ds(1, layers), middle], out_hbm.at[0], out_sem)
    written.start()
    sent = []
    for number in range(len(groups)):
        for k, copy in enumerate(started):
            copy.wait_recv()
            total = total + sums[number][k]
        sent += started
        if number + 1 < len(groups):
            partial[number + 1] = total
            started = exchange(number + 1)
    for number in range(ITERS):
        part = jnp.sum(jnp.where(low // 4 == number, total, 0.0))
        root = jnp.sqrt(jnp.broadcast_to(part, (8, lanes)))
        trace[number] = root[0, 0]

    for condition, copy in copies:

        @pl.when(condition)
        def _():
            copy.wait_send()

    for copy in sent:
        copy.wait_send()
    across.wait_send()
    written.wait()


def on_device(sizes, source, classes, table):
    layers, rows, lanes = source.shape[1:]
    wide = rows + 2 * REACH
    groups = reduce_groups(sizes)
    counts = []
    for group in groups:
        count = 1
        for axis in group:
            count *= sizes[axis]
        counts.append(count)
    near = wide - 2 * SWEEPS
    return pl.pallas_call(
        functools.partial(kernel, sizes),
        out_shape=(
            jax.ShapeDtypeStruct(source.shape, jnp.float32),
            jax.ShapeDtypeStruct((ITERS,), jnp.float32),
        ),
        in_specs=[
            pl.BlockSpec(memory_space=pltpu.HBM),
            pl.BlockSpec(memory_space=pltpu.HBM),
            pl.BlockSpec(memory_space=pltpu.HBM),
        ],
        out_specs=(
            pl.BlockSpec(memory_space=pl.ANY),
            pl.BlockSpec(memory_space=pltpu.SMEM),
        ),
        scratch_shapes=[
            pltpu.VMEM((layers, wide, lanes), jnp.float32),
            pltpu.VMEM((layers, wide, lanes), jnp.int32),
            pltpu.VMEM((2, rows, lanes), jnp.float32),
            pltpu.VMEM((2, wide, lanes), jnp.float32),
            pltpu.VMEM((4, 2, layers, wide, lanes), jnp.float32),
            pltpu.VMEM((2, 2, layers + 2, wide, lanes), jnp.float32),
            pltpu.VMEM((2, wide, lanes), jnp.float32),
            pltpu.VMEM((2, near, lanes), jnp.float32),
            pltpu.VMEM((2, near, lanes), jnp.float32),
            *[pltpu.VMEM((count - 1, 8, lanes), jnp.float32) for count in counts],
            pltpu.VMEM((len(groups), 8, lanes), jnp.float32),
            pltpu.SMEM((3, 2, NCLASS), jnp.float32),
            pltpu.SemaphoreType.DMA((3,)),
            pltpu.SemaphoreType.DMA((10,)),
            pltpu.SemaphoreType.DMA((10,)),
            pltpu.SemaphoreType.DMA((2,)),
            pltpu.SemaphoreType.DMA((len(groups), max(counts))),
            pltpu.SemaphoreType.DMA((len(groups), max(counts))),
            pltpu.SemaphoreType.DMA,
        ],
        compiler_params=pltpu.CompilerParams(
            collective_id=0, has_side_effects=True, vmem_limit_bytes=64 * 2**20
        ),
    )(source, classes, table.transpose(2, 0, 1))


def solution(mesh):
    sizes = {axis: mesh.shape[axis] for axis in AXES}
    in_specs = (P("side", None, "gx", "gy"), P("side", None, "gx", "gy"), P())
    out_specs = (P("side", None, "gx", "gy"), P())
    return jax.shard_map(
        functools.partial(on_device, sizes),
        mesh=mesh,
        in_specs=in_specs,
        out_specs=out_specs,
        check_vma=False,
    )
```

```python
import functools

import jax
import jax.numpy as jnp
from jax import lax
from jax.experimental import pallas as pl
from jax.experimental.pallas import tpu as pltpu
from jax.sharding import PartitionSpec as P

SWEEPS = 8
ITERS = 2
NCLASS = 8
REACH = SWEEPS * ITERS

relax_weight = 0.8
robin_weight = 2.0

MESH = pl.DeviceIdType.MESH
AXES = ("gx", "gy", "side")
AROUND = [(dx, dy) for dx in (-1, 0, 1) for dy in (-1, 0, 1) if (dx, dy) != (0, 0)]


def reduce_groups(sizes):
    if sizes["gx"] * sizes["gy"] * sizes["side"] <= 64:
        return [("gx", "gy", "side")]
    return [("gx", "side"), ("gy",)]


def kernel(
    sizes,
    source_hbm,
    classes_hbm,
    table_hbm,
    out_hbm,
    totals,
    src,
    cls,
    pack,
    halo,
    cond,
    field,
    weight,
    mine,
    theirs,
    *rest,
):
    groups = reduce_groups(sizes)
    sums = rest[: len(groups)]
    partial, table, local_sem, send_sem, recv_sem, side_sem, sum_send, sum_recv, out_sem = rest[len(groups) :]
    layers, rows, lanes = source_hbm.shape[1:]
    wide = rows + 2 * REACH
    gx, gy, side = (lax.axis_index(axis) for axis in AXES)
    at = {"gx": gx, "gy": gy, "side": side}

    def exists(dx, dy):
        ok = None
        for d, axis in ((dx, "gx"), (dy, "gy")):
            if d:
                here = at[axis] > 0 if d < 0 else at[axis] < sizes[axis] - 1
                ok = here if ok is None else ok & here
        return ok

    def members(group):
        places = [{}]
        for axis in group:
            turned = [at[axis]]
            for step in range(1, sizes[axis]):
                turned.append(jnp.where(at[axis] >= sizes[axis] - step, at[axis] + (step - sizes[axis]), at[axis] + step))
            places = [{**place, axis: here} for place in places for here in turned]
        return [tuple({**at, **place}[axis] for axis in AXES) for place in places[1:]]

    peers_of = [members(group) for group in groups]

    load_table = pltpu.make_async_copy(table_hbm, table, local_sem.at[2])
    load_table.start()
    middle = pl.ds(REACH, rows)
    load_src = pltpu.make_async_copy(source_hbm.at[0], src.at[:, middle], local_sem.at[0])
    load_cls = pltpu.make_async_copy(classes_hbm.at[0], cls.at[:, middle], local_sem.at[1])
    load_src.start()
    load_cls.start()

    barrier = pltpu.get_barrier_semaphore()
    expected = 1
    pl.semaphore_signal(barrier, inc=1, device_id=(gx, gy, 1 - side), device_id_type=MESH)
    for dx, dy in AROUND:
        ok = exists(dx, dy)
        expected = expected + ok.astype(jnp.int32)

        @pl.when(ok)
        def _():
            pl.semaphore_signal(barrier, inc=1, device_id=(gx + dx, gy + dy, side), device_id_type=MESH)

    for peers in peers_of:
        for peer in peers:
            pl.semaphore_signal(barrier, inc=1, device_id=peer, device_id_type=MESH)
            expected = expected + 1

    lane = lax.broadcasted_iota(jnp.int32, (8, lanes), 1)
    load_table.wait()
    scalars = [[table[column, side, level] for column in range(3)] for level in range(NCLASS)]
    columns = []
    for column in range(3):
        value = jnp.zeros((8, lanes), jnp.float32)
        for level in range(NCLASS):
            value = jnp.where(lane == level, scalars[level][column], value)
        columns.append(value)
    doubled = 2.0 * (columns[0] + columns[1] + columns[2])
    doubled = jnp.where(lane < NCLASS, doubled, 1.0)
    tables = []
    for extra in (robin_weight, 0.0):
        share = relax_weight / (doubled + extra)
        tables.append([share * column for column in columns] + [share])

    load_src.wait()
    load_cls.wait()

    lane_wide = lax.broadcasted_iota(jnp.int32, (rows, lanes), 1)
    for way, first in ((0, 0), (1, lanes - REACH)):
        packed = jnp.zeros((rows, lanes), jnp.float32)
        for strip in range(2 * layers):
            ref = src if strip < layers else cls
            value = ref[strip % layers, middle, :].astype(jnp.float32)
            shift = (strip * REACH - first) % lanes
            if shift:
                value = pltpu.roll(value, shift, 1)
            packed = jnp.where(lane_wide // REACH == strip, value, packed)
        pack[way] = packed

    pl.semaphore_wait(barrier, expected)

    copies = []

    def send(condition, source_ref, target_ref, peer):
        number = len(copies)
        copy = pltpu.make_async_remote_copy(
            src_ref=source_ref,
            dst_ref=target_ref,
            send_sem=send_sem.at[number],
            recv_sem=recv_sem.at[number],
            device_id=peer,
            device_id_type=MESH,
        )
        copies.append((condition, copy))

        @pl.when(condition)
        def _():
            copy.start()

    def strip_of(dx):
        if dx == 0:
            return middle, pl.ds(0, rows), middle
        if dx > 0:
            return pl.ds(rows, REACH), pl.ds(rows - REACH, REACH), pl.ds(0, REACH)
        return pl.ds(REACH, REACH), pl.ds(0, REACH), pl.ds(REACH + rows, REACH)

    arrive = []
    for dx, dy in sorted(AROUND, key=lambda d: -abs(d[0]) - abs(d[1])):
        held, inner, landing = strip_of(dx)
        peer = (gx + dx, gy + dy, side)
        arrive.append(exists(-dx, -dy))
        if dy == 0:
            send(exists(dx, dy), src.at[:, held], src.at[:, landing], peer)
            arrive.append(exists(-dx, -dy))
            send(exists(dx, dy), cls.at[:, held], cls.at[:, landing], peer)
        elif dy > 0:
            send(exists(dx, dy), pack.at[1, inner], halo.at[0, landing], peer)
        else:
            send(exists(dx, dy), pack.at[0, inner], halo.at[1, landing], peer)

    def lookup(kinds, wanted):
        chosen = []
        for row in wanted:
            chosen.append(jnp.take_along_axis(jnp.broadcast_to(row[:1], kinds.shape), kinds, axis=1))
        return chosen

    def settle(part, layer, span, kinds, values, ok):
        count = span.size
        wanted = lookup(kinds, tables[0 if layer == 0 else 1])
        wanted[3], values = wanted[3], wanted[3] * values
        if ok is not None:
            wanted = [jnp.where(ok, value, 0.0) for value in wanted]
            values = jnp.where(ok, values, 0.0)
        for number in range(3):
            cond[number, part, layer, span] = wanted[number]
        cond[3, part, layer, span] = values
        field[1, part, layer + 1, span] = values
        if layer == 0:
            weight[part, span] = wanted[3]

    zero = jnp.zeros((wide, lanes), jnp.float32)
    for slot in range(2):
        for part in range(2):
            field[slot, part, 0] = zero
            field[slot, part, layers + 1] = zero

    for layer in range(layers):
        settle(0, layer, middle, cls[layer, middle, :], src[layer, middle, :], None)

    for (condition, copy), here in zip(copies, arrive):

        @pl.when(here)
        def _():
            copy.wait_recv()

    for dx in (-1, 1):
        span = pl.ds(0, REACH) if dx < 0 else pl.ds(REACH + rows, REACH)
        there = exists(dx, 0)
        ok = jnp.broadcast_to(there, (REACH, lanes))
        for layer in range(layers):
            settle(0, layer, span, jnp.where(ok, cls[layer, span, :], 0), src[layer, span, :], ok)

    row = lax.broadcasted_iota(jnp.int32, (wide, lanes), 0)
    wide_lane = lax.broadcasted_iota(jnp.int32, (wide, lanes), 1)
    ok_rows = ((row >= REACH) | (gx > 0)) & ((row < REACH + rows) | (gx < sizes["gx"] - 1))
    ok_left = ok_rows & (wide_lane >= lanes - REACH) & (gy > 0)
    ok_right = ok_rows & (wide_lane < REACH) & (gy < sizes["gy"] - 1)
    ok_wide = ok_left | ok_right
    halo_left = halo[0]
    halo_right = halo[1]
    everything = pl.ds(0, wide)
    for layer in range(layers):
        found = []
        for strip in (layer, layers + layer):
            left = pltpu.roll(halo_left, (lanes - REACH - strip * REACH) % lanes, 1)
            right = pltpu.roll(halo_right, (-strip * REACH) % lanes, 1) if strip else halo_right
            found.append(jnp.where(ok_left, left, jnp.where(ok_right, right, 0.0)))
        settle(1, layer, everything, found[1].astype(jnp.int32), found[0], ok_wide)

    def relax(time, layer, first, count, parts=2):
        old, new = (time - 1) % 2, time % 2
        span = pl.ds(first, count)
        edge = lax.broadcasted_iota(jnp.int32, (count, lanes), 1)
        grow = REACH if parts == 1 else 0
        before = [field[old, part, layer + 1, span] for part in range(2)]
        from_left = [pltpu.roll(value, 1, 1) for value in before]
        from_right = [pltpu.roll(value, lanes - 1, 1) for value in before]
        for part in range(parts):
            here = before[part]
            if parts == 1:
                outer = field[old, part, layer + 1, pl.ds(first - 8, count + 16)]
                above = pltpu.roll(outer, 1, 0)[8 : 8 + count]
                below = pltpu.roll(outer, count + 15, 0)[8 : 8 + count]
            else:
                above = pltpu.roll(here, 1, 0)
                below = pltpu.roll(here, count - 1, 0)
            left = jnp.where(edge == 0, from_left[1 - part], from_left[part])
            right = jnp.where(edge == lanes - 1, from_right[1 - part], from_right[part])
            deep = field[old, part, layer, span] + field[old, part, layer + 2, span]
            value = (1.0 - relax_weight) * here + cond[3, part, layer, span]
            value = value + cond[0, part, layer, span] * (above + below)
            value = value + cond[1, part, layer, span] * (left + right)
            value = value + cond[2, part, layer, span] * deep
            field[new, part, layer + 1, span] = value

    def sweep(time, layer):
        if time <= SWEEPS:
            relax(time, layer, 0, wide)
        elif time < REACH:
            relax(time, layer, SWEEPS, wide - 2 * SWEEPS)
        else:
            relax(time, layer, REACH, rows, parts=1)

    def full(start, pairs):
        @pl.loop(0, pairs)
        def _(_):
            for time in (start, start + 1):
                for layer in range(layers):
                    sweep(time, layer)

    def head(last):
        for depth in range(layers - 1):
            time = last - (layers - 2) + depth
            for layer in range(layers - 1 - depth):
                sweep(time, layer)

    def tail(last):
        for step in range(layers - 1):
            for layer in range(layers - 1, step, -1):
                sweep(last - layer + 1 + step, layer)

    full(2, 2)
    head(SWEEPS)
    near = pl.ds(SWEEPS, wide - 2 * SWEEPS)
    for part in range(2):
        mine[part] = robin_weight * field[0, part, 1, near]
    across = pltpu.make_async_remote_copy(
        src_ref=mine,
        dst_ref=theirs,
        send_sem=side_sem.at[0],
        recv_sem=side_sem.at[1],
        device_id=(gx, gy, 1 - side),
        device_id_type=MESH,
    )
    across.start()
    tail(SWEEPS)

    for depth in range(layers - 1):
        for layer in range(1 + depth, layers):
            sweep(SWEEPS + 1 + depth, layer)
    across.wait_recv()
    for part in range(2):
        cond[3, part, 0, near] = cond[3, part, 0, near] + weight[part, near] * theirs[part]
    for depth in range(layers - 1):
        for layer in range(layers - 1 - depth):
            sweep(SWEEPS + 1 + depth + layer, layer)
    full(SWEEPS + layers, 1)
    head(REACH)

    inner = pl.ds(SWEEPS, rows)
    first_change = mine[0, inner]
    own = robin_weight * field[0, 0, 1, middle]
    second_change = own - theirs[0, inner] - first_change
    folded = []
    for change in (first_change, second_change):
        square = jnp.sum(change * change, axis=0, keepdims=True)
        folded.append(square + pltpu.roll(square, lanes // 2, 1))
    total = jnp.where(lane[:1] < lanes // 2, folded[0], folded[1])

    def exchange(number):
        slots = sums[number]
        peers = peers_of[number]
        started = []
        for k, peer in enumerate(peers):
            copy = pltpu.make_async_remote_copy(
                src_ref=partial.at[number],
                dst_ref=slots.at[k],
                send_sem=sum_send.at[number, k],
                recv_sem=sum_recv.at[number, k],
                device_id=peer,
                device_id_type=MESH,
            )
            copy.start()
            started.append(copy)
        return started

    partial[0] = total
    started = exchange(0)
    tail(REACH)
    written = pltpu.make_async_copy(field.at[0, 0, pl.ds(1, layers), middle], out_hbm.at[0], out_sem)
    written.start()
    sent = []
    for number in range(len(groups)):
        for k, copy in enumerate(started):
            copy.wait_recv()
            total = total + sums[number][k]
        sent += started
        if number + 1 < len(groups):
            partial[number + 1] = total
            started = exchange(number + 1)
    totals[...] = total
    for condition, copy in copies:

        @pl.when(condition)
        def _():
            copy.wait_send()

    for copy in sent:
        copy.wait_send()
    across.wait_send()
    written.wait()


def finish(held, totals, out_hbm, trace, sem):
    copy = pltpu.make_async_copy(held, out_hbm, sem)
    copy.start()
    total = totals[...]
    half = total.shape[1] // 2
    lane = lax.broadcasted_iota(jnp.int32, total.shape, 1)
    for number in range(ITERS):
        part = jnp.sum(jnp.where(lane // half == number, total, 0.0))
        root = jnp.sqrt(jnp.broadcast_to(part, total.shape))
        trace[number] = root[0, 0]
    copy.wait()


def on_device(sizes, source, classes, table):
    layers, rows, lanes = source.shape[1:]
    wide = rows + 2 * REACH
    groups = reduce_groups(sizes)
    counts = []
    for group in groups:
        count = 1
        for axis in group:
            count *= sizes[axis]
        counts.append(count)
    near = wide - 2 * SWEEPS
    held, totals = pl.pallas_call(
        functools.partial(kernel, sizes),
        out_shape=(
            pltpu.VMEM(source.shape, jnp.float32),
            pltpu.VMEM((1, lanes), jnp.float32),
        ),
        in_specs=[
            pl.BlockSpec(memory_space=pltpu.HBM),
            pl.BlockSpec(memory_space=pltpu.HBM),
            pl.BlockSpec(memory_space=pltpu.HBM),
        ],
        out_specs=(
            pl.BlockSpec(memory_space=pl.ANY),
            pl.BlockSpec(memory_space=pltpu.VMEM),
        ),
        scratch_shapes=[
            pltpu.VMEM((layers, wide, lanes), jnp.float32),
            pltpu.VMEM((layers, wide, lanes), jnp.int32),
            pltpu.VMEM((2, rows, lanes), jnp.float32),
            pltpu.VMEM((2, wide, lanes), jnp.float32),
            pltpu.VMEM((4, 2, layers, wide, lanes), jnp.float32),
            pltpu.VMEM((2, 2, layers + 2, wide, lanes), jnp.float32),
            pltpu.VMEM((2, wide, lanes), jnp.float32),
            pltpu.VMEM((2, near, lanes), jnp.float32),
            pltpu.VMEM((2, near, lanes), jnp.float32),
            *[pltpu.VMEM((count - 1, 1, lanes), jnp.float32) for count in counts],
            pltpu.VMEM((len(groups), 1, lanes), jnp.float32),
            pltpu.SMEM((3, 2, NCLASS), jnp.float32),
            pltpu.SemaphoreType.DMA((3,)),
            pltpu.SemaphoreType.DMA((10,)),
            pltpu.SemaphoreType.DMA((10,)),
            pltpu.SemaphoreType.DMA((2,)),
            pltpu.SemaphoreType.DMA((len(groups), max(counts))),
            pltpu.SemaphoreType.DMA((len(groups), max(counts))),
            pltpu.SemaphoreType.DMA,
        ],
        compiler_params=pltpu.CompilerParams(
            collective_id=0, has_side_effects=True, vmem_limit_bytes=48 * 2**20
        ),
    )(
        pltpu.with_memory_space_constraint(source, pltpu.HBM),
        pltpu.with_memory_space_constraint(classes, pltpu.HBM),
        pltpu.with_memory_space_constraint(table.transpose(2, 0, 1), pltpu.HBM),
    )
    return pl.pallas_call(
        finish,
        out_shape=(
            jax.ShapeDtypeStruct(source.shape, jnp.float32),
            jax.ShapeDtypeStruct((ITERS,), jnp.float32),
        ),
        in_specs=[pl.BlockSpec(memory_space=pl.ANY), pl.BlockSpec(memory_space=pltpu.VMEM)],
        out_specs=(pl.BlockSpec(memory_space=pltpu.HBM), pl.BlockSpec(memory_space=pltpu.SMEM)),
        scratch_shapes=[pltpu.SemaphoreType.DMA],
        compiler_params=pltpu.CompilerParams(vmem_limit_bytes=2**20),
    )(held, totals)


def solution(mesh):
    sizes = {axis: mesh.shape[axis] for axis in AXES}
    in_specs = (P("side", None, "gx", "gy"), P("side", None, "gx", "gy"), P())
    out_specs = (P("side", None, "gx", "gy"), P())
    return jax.shard_map(
        functools.partial(on_device, sizes),
        mesh=mesh,
        in_specs=in_specs,
        out_specs=out_specs,
        check_vma=False,
    )
```

```python
import functools

import jax
import jax.numpy as jnp
from jax import lax
from jax.experimental import pallas as pl
from jax.experimental.pallas import tpu as pltpu
from jax.sharding import PartitionSpec as P

SWEEPS = 8
ITERS = 2
NCLASS = 8
REACH = SWEEPS * ITERS

relax_weight = 0.8
robin_weight = 2.0

MESH = pl.DeviceIdType.MESH
AXES = ("gx", "gy", "side")
AROUND = [(dx, dy) for dx in (-1, 0, 1) for dy in (-1, 0, 1) if (dx, dy) != (0, 0)]


def reduce_groups(sizes):
    if sizes["gx"] * sizes["gy"] * sizes["side"] <= 64:
        return [("gx", "gy", "side")]
    return [("gx", "side"), ("gy",)]


def kernel(
    sizes,
    source_hbm,
    classes_hbm,
    table_hbm,
    out_hbm,
    totals,
    src,
    cls,
    pack,
    halo,
    cond,
    field,
    weight,
    mine,
    theirs,
    *rest,
):
    groups = reduce_groups(sizes)
    sums = rest[: len(groups)]
    partial, table, local_sem, send_sem, recv_sem, side_sem, sum_send, sum_recv, out_sem = rest[len(groups) :]
    layers, rows, lanes = source_hbm.shape[1:]
    wide = rows + 2 * REACH
    gx, gy, side = (lax.axis_index(axis) for axis in AXES)
    at = {"gx": gx, "gy": gy, "side": side}

    def exists(dx, dy):
        ok = None
        for d, axis in ((dx, "gx"), (dy, "gy")):
            if d:
                here = at[axis] > 0 if d < 0 else at[axis] < sizes[axis] - 1
                ok = here if ok is None else ok & here
        return ok

    def members(group):
        places = [{}]
        for axis in group:
            turned = [at[axis]]
            for step in range(1, sizes[axis]):
                turned.append(jnp.where(at[axis] >= sizes[axis] - step, at[axis] + (step - sizes[axis]), at[axis] + step))
            places = [{**place, axis: here} for place in places for here in turned]
        return [tuple({**at, **place}[axis] for axis in AXES) for place in places[1:]]

    peers_of = [members(group) for group in groups]

    load_table = pltpu.make_async_copy(table_hbm, table, local_sem.at[2])
    load_table.start()
    middle = pl.ds(REACH, rows)
    load_src = pltpu.make_async_copy(source_hbm.at[0], src.at[:, middle], local_sem.at[0])
    load_cls = pltpu.make_async_copy(classes_hbm.at[0], cls.at[:, middle], local_sem.at[1])
    load_src.start()
    load_cls.start()

    barrier = pltpu.get_barrier_semaphore()
    expected = 1
    pl.semaphore_signal(barrier, inc=1, device_id=(gx, gy, 1 - side), device_id_type=MESH)
    for dx, dy in AROUND:
        ok = exists(dx, dy)
        expected = expected + ok.astype(jnp.int32)

        @pl.when(ok)
        def _():
            pl.semaphore_signal(barrier, inc=1, device_id=(gx + dx, gy + dy, side), device_id_type=MESH)

    for peers in peers_of:
        for peer in peers:
            pl.semaphore_signal(barrier, inc=1, device_id=peer, device_id_type=MESH)
            expected = expected + 1

    lane = lax.broadcasted_iota(jnp.int32, (8, lanes), 1)
    load_table.wait()
    scalars = [[table[column, side, level] for column in range(3)] for level in range(NCLASS)]
    columns = []
    for column in range(3):
        value = jnp.zeros((8, lanes), jnp.float32)
        for level in range(NCLASS):
            value = jnp.where(lane == level, scalars[level][column], value)
        columns.append(value)
    doubled = 2.0 * (columns[0] + columns[1] + columns[2])
    doubled = jnp.where(lane < NCLASS, doubled, 1.0)
    tables = []
    for extra in (robin_weight, 0.0):
        share = relax_weight / (doubled + extra)
        tables.append([share * column for column in columns] + [share])

    load_src.wait()
    load_cls.wait()

    lane_wide = lax.broadcasted_iota(jnp.int32, (rows, lanes), 1)
    for way, first in ((0, 0), (1, lanes - REACH)):
        packed = jnp.zeros((rows, lanes), jnp.float32)
        for strip in range(2 * layers):
            ref = src if strip < layers else cls
            value = ref[strip % layers, middle, :].astype(jnp.float32)
            shift = (strip * REACH - first) % lanes
            if shift:
                value = pltpu.roll(value, shift, 1)
            packed = jnp.where(lane_wide // REACH == strip, value, packed)
        pack[way] = packed

    pl.semaphore_wait(barrier, expected)

    copies = []

    def send(condition, source_ref, target_ref, peer):
        number = len(copies)
        copy = pltpu.make_async_remote_copy(
            src_ref=source_ref,
            dst_ref=target_ref,
            send_sem=send_sem.at[number],
            recv_sem=recv_sem.at[number],
            device_id=peer,
            device_id_type=MESH,
        )
        copies.append((condition, copy))

        @pl.when(condition)
        def _():
            copy.start()

    def strip_of(dx):
        if dx == 0:
            return middle, pl.ds(0, rows), middle
        if dx > 0:
            return pl.ds(rows, REACH), pl.ds(rows - REACH, REACH), pl.ds(0, REACH)
        return pl.ds(REACH, REACH), pl.ds(0, REACH), pl.ds(REACH + rows, REACH)

    arrive = []
    for dx, dy in sorted(AROUND, key=lambda d: -abs(d[0]) - abs(d[1])):
        held, inner, landing = strip_of(dx)
        peer = (gx + dx, gy + dy, side)
        arrive.append(exists(-dx, -dy))
        if dy == 0:
            send(exists(dx, dy), src.at[:, held], src.at[:, landing], peer)
            arrive.append(exists(-dx, -dy))
            send(exists(dx, dy), cls.at[:, held], cls.at[:, landing], peer)
        elif dy > 0:
            send(exists(dx, dy), pack.at[1, inner], halo.at[0, landing], peer)
        else:
            send(exists(dx, dy), pack.at[0, inner], halo.at[1, landing], peer)

    def lookup(kinds, wanted):
        chosen = []
        for row in wanted:
            chosen.append(jnp.take_along_axis(jnp.broadcast_to(row[:1], kinds.shape), kinds, axis=1))
        return chosen

    def settle(part, layer, span, kinds, values, ok):
        count = span.size
        wanted = lookup(kinds, tables[0 if layer == 0 else 1])
        wanted[3], values = wanted[3], wanted[3] * values
        if ok is not None:
            wanted = [jnp.where(ok, value, 0.0) for value in wanted]
            values = jnp.where(ok, values, 0.0)
        for number in range(3):
            cond[number, part, layer, span] = wanted[number]
        cond[3, part, layer, span] = values
        field[1, part, layer + 1, span] = values
        if layer == 0:
            weight[part, span] = wanted[3]

    zero = jnp.zeros((wide, lanes), jnp.float32)
    for slot in range(2):
        for part in range(2):
            field[slot, part, 0] = zero
            field[slot, part, layers + 1] = zero

    for layer in range(layers):
        settle(0, layer, middle, cls[layer, middle, :], src[layer, middle, :], None)

    for (condition, copy), here in zip(copies, arrive):

        @pl.when(here)
        def _():
            copy.wait_recv()

    for dx in (-1, 1):
        span = pl.ds(0, REACH) if dx < 0 else pl.ds(REACH + rows, REACH)
        there = exists(dx, 0)
        ok = jnp.broadcast_to(there, (REACH, lanes))
        for layer in range(layers):
            settle(0, layer, span, jnp.where(ok, cls[layer, span, :], 0), src[layer, span, :], ok)

    row = lax.broadcasted_iota(jnp.int32, (wide, lanes), 0)
    wide_lane = lax.broadcasted_iota(jnp.int32, (wide, lanes), 1)
    ok_rows = ((row >= REACH) | (gx > 0)) & ((row < REACH + rows) | (gx < sizes["gx"] - 1))
    ok_left = ok_rows & (wide_lane >= lanes - REACH) & (gy > 0)
    ok_right = ok_rows & (wide_lane < REACH) & (gy < sizes["gy"] - 1)
    ok_wide = ok_left | ok_right
    halo_left = halo[0]
    halo_right = halo[1]
    everything = pl.ds(0, wide)
    for layer in range(layers):
        found = []
        for strip in (layer, layers + layer):
            left = pltpu.roll(halo_left, (lanes - REACH - strip * REACH) % lanes, 1)
            right = pltpu.roll(halo_right, (-strip * REACH) % lanes, 1) if strip else halo_right
            found.append(jnp.where(ok_left, left, jnp.where(ok_right, right, 0.0)))
        settle(1, layer, everything, found[1].astype(jnp.int32), found[0], ok_wide)

    def relax(time, layer, first, count, parts=2):
        old, new = (time - 1) % 2, time % 2
        span = pl.ds(first, count)
        edge = lax.broadcasted_iota(jnp.int32, (count, lanes), 1)
        grow = REACH if parts == 1 else 0
        before = [field[old, part, layer + 1, span] for part in range(2)]
        from_left = [pltpu.roll(value, 1, 1) for value in before]
        from_right = [pltpu.roll(value, lanes - 1, 1) for value in before]
        for part in range(parts):
            here = before[part]
            if parts == 1:
                outer = field[old, part, layer + 1, pl.ds(first - 8, count + 16)]
                above = pltpu.roll(outer, 1, 0)[8 : 8 + count]
                below = pltpu.roll(outer, count + 15, 0)[8 : 8 + count]
            else:
                above = pltpu.roll(here, 1, 0)
                below = pltpu.roll(here, count - 1, 0)
            left = jnp.where(edge == 0, from_left[1 - part], from_left[part])
            right = jnp.where(edge == lanes - 1, from_right[1 - part], from_right[part])
            deep = field[old, part, layer, span] + field[old, part, layer + 2, span]
            value = (1.0 - relax_weight) * here + cond[3, part, layer, span]
            value = value + cond[0, part, layer, span] * (above + below)
            value = value + cond[1, part, layer, span] * (left + right)
            value = value + cond[2, part, layer, span] * deep
            field[new, part, layer + 1, span] = value

    def sweep(time, layer):
        if time <= SWEEPS:
            relax(time, layer, 0, wide)
        elif time < REACH:
            relax(time, layer, SWEEPS, wide - 2 * SWEEPS)
        else:
            relax(time, layer, REACH, rows, parts=1)

    def full(start, pairs):
        @pl.loop(0, pairs)
        def _(_):
            for time in (start, start + 1):
                for layer in range(layers):
                    sweep(time, layer)

    def head(last):
        for depth in range(layers - 1):
            time = last - (layers - 2) + depth
            for layer in range(layers - 1 - depth):
                sweep(time, layer)

    def tail(last):
        for step in range(layers - 1):
            for layer in range(layers - 1, step, -1):
                sweep(last - layer + 1 + step, layer)

    full(2, 2)
    head(SWEEPS)
    near = pl.ds(SWEEPS, wide - 2 * SWEEPS)
    for part in range(2):
        mine[part] = robin_weight * field[0, part, 1, near]
    across = pltpu.make_async_remote_copy(
        src_ref=mine,
        dst_ref=theirs,
        send_sem=side_sem.at[0],
        recv_sem=side_sem.at[1],
        device_id=(gx, gy, 1 - side),
        device_id_type=MESH,
    )
    across.start()
    tail(SWEEPS)

    for depth in range(layers - 1):
        for layer in range(1 + depth, layers):
            sweep(SWEEPS + 1 + depth, layer)
    across.wait_recv()
    for part in range(2):
        cond[3, part, 0, near] = cond[3, part, 0, near] + weight[part, near] * theirs[part]
    for depth in range(layers - 1):
        for layer in range(layers - 1 - depth):
            sweep(SWEEPS + 1 + depth + layer, layer)
    full(SWEEPS + layers, 1)
    head(REACH)

    inner = pl.ds(SWEEPS, rows)
    first_change = mine[0, inner]
    own = robin_weight * field[0, 0, 1, middle]
    second_change = own - theirs[0, inner] - first_change
    folded = []
    for change in (first_change, second_change):
        square = jnp.sum(change * change, axis=0, keepdims=True)
        folded.append(square + pltpu.roll(square, lanes // 2, 1))
    total = jnp.where(lane[:1] < lanes // 2, folded[0], folded[1])

    def exchange(number):
        slots = sums[number]
        peers = peers_of[number]
        started = []
        for k, peer in enumerate(peers):
            copy = pltpu.make_async_remote_copy(
                src_ref=partial.at[number],
                dst_ref=slots.at[k],
                send_sem=sum_send.at[number, k],
                recv_sem=sum_recv.at[number, k],
                device_id=peer,
                device_id_type=MESH,
            )
            copy.start()
            started.append(copy)
        return started

    partial[0] = total
    started = exchange(0)
    tail(REACH)
    written = pltpu.make_async_copy(field.at[0, 0, pl.ds(1, layers), middle], out_hbm.at[0], out_sem)
    written.start()
    for condition, copy in copies:

        @pl.when(condition)
        def _():
            copy.wait_send()

    across.wait_send()
    written.wait()
    sent = []
    for number in range(len(groups)):
        for k, copy in enumerate(started):
            copy.wait_recv()
            total = total + sums[number][k]
        sent += started
        if number + 1 < len(groups):
            partial[number + 1] = total
            started = exchange(number + 1)
    totals[...] = total
    for copy in sent:
        copy.wait_send()


def finish(held, totals, out_hbm, trace_hbm, trace, sem):
    copy = pltpu.make_async_copy(held, out_hbm, sem.at[0])
    copy.start()
    total = totals[...]
    half = total.shape[1] // 2
    lane = lax.broadcasted_iota(jnp.int32, total.shape, 1)
    for number in range(ITERS):
        part = jnp.sum(jnp.where(lane // half == number, total, 0.0))
        root = jnp.sqrt(jnp.broadcast_to(part, total.shape))
        trace[number] = root[0, 0]
    small = pltpu.make_async_copy(trace, trace_hbm, sem.at[1])
    small.start()
    small.wait()
    copy.wait()


def on_device(sizes, source, classes, table):
    layers, rows, lanes = source.shape[1:]
    wide = rows + 2 * REACH
    groups = reduce_groups(sizes)
    counts = []
    for group in groups:
        count = 1
        for axis in group:
            count *= sizes[axis]
        counts.append(count)
    near = wide - 2 * SWEEPS
    held, totals = pl.pallas_call(
        functools.partial(kernel, sizes),
        out_shape=(
            pltpu.VMEM(source.shape, jnp.float32),
            pltpu.VMEM((1, lanes), jnp.float32),
        ),
        in_specs=[
            pl.BlockSpec(memory_space=pltpu.HBM),
            pl.BlockSpec(memory_space=pltpu.HBM),
            pl.BlockSpec(memory_space=pltpu.HBM),
        ],
        out_specs=(
            pl.BlockSpec(memory_space=pl.ANY),
            pl.BlockSpec(memory_space=pltpu.VMEM),
        ),
        scratch_shapes=[
            pltpu.VMEM((layers, wide, lanes), jnp.float32),
            pltpu.VMEM((layers, wide, lanes), jnp.int32),
            pltpu.VMEM((2, rows, lanes), jnp.float32),
            pltpu.VMEM((2, wide, lanes), jnp.float32),
            pltpu.VMEM((4, 2, layers, wide, lanes), jnp.float32),
            pltpu.VMEM((2, 2, layers + 2, wide, lanes), jnp.float32),
            pltpu.VMEM((2, wide, lanes), jnp.float32),
            pltpu.VMEM((2, near, lanes), jnp.float32),
            pltpu.VMEM((2, near, lanes), jnp.float32),
            *[pltpu.VMEM((count - 1, 1, lanes), jnp.float32) for count in counts],
            pltpu.VMEM((len(groups), 1, lanes), jnp.float32),
            pltpu.SMEM((3, 2, NCLASS), jnp.float32),
            pltpu.SemaphoreType.DMA((3,)),
            pltpu.SemaphoreType.DMA((10,)),
            pltpu.SemaphoreType.DMA((10,)),
            pltpu.SemaphoreType.DMA((2,)),
            pltpu.SemaphoreType.DMA((len(groups), max(counts))),
            pltpu.SemaphoreType.DMA((len(groups), max(counts))),
            pltpu.SemaphoreType.DMA,
        ],
        compiler_params=pltpu.CompilerParams(
            collective_id=0, has_side_effects=True, vmem_limit_bytes=48 * 2**20
        ),
    )(
        pltpu.with_memory_space_constraint(source, pltpu.HBM),
        pltpu.with_memory_space_constraint(classes, pltpu.HBM),
        pltpu.with_memory_space_constraint(table.transpose(2, 0, 1), pltpu.HBM),
    )
    return pl.pallas_call(
        finish,
        out_shape=(
            jax.ShapeDtypeStruct(source.shape, jnp.float32),
            jax.ShapeDtypeStruct((ITERS,), jnp.float32),
        ),
        in_specs=[pl.BlockSpec(memory_space=pl.ANY), pl.BlockSpec(memory_space=pltpu.VMEM)],
        out_specs=(pl.BlockSpec(memory_space=pltpu.HBM), pl.BlockSpec(memory_space=pltpu.HBM)),
        scratch_shapes=[pltpu.SMEM((ITERS,), jnp.float32), pltpu.SemaphoreType.DMA((2,))],
        compiler_params=pltpu.CompilerParams(vmem_limit_bytes=2**20),
    )(held, totals)


def solution(mesh):
    sizes = {axis: mesh.shape[axis] for axis in AXES}
    in_specs = (P("side", None, "gx", "gy"), P("side", None, "gx", "gy"), P())
    out_specs = (P("side", None, "gx", "gy"), P())
    return jax.shard_map(
        functools.partial(on_device, sizes),
        mesh=mesh,
        in_specs=in_specs,
        out_specs=out_specs,
        check_vma=False,
    )
```
